32 devices in a mesh: pipe: 8 (over z, core), tensor: 4 (over y, x).
Axes of the slice: x: 2, y: 2, z: 4, core: 2. Of those that a mesh axis runs over, the one named last changes fastest.
Arguments:
- held_rows: bfloat16 [8, 512, 2688], P('pipe', 'tensor'), may hold values from -6 to 6
- incoming: bfloat16 [1, 512, 2688], P(None, 'tensor'), may hold values from -6 to 6
- first_position: int32 [1], replicated, may hold values from 0 to 511
- in_gain: float32 [8, 2688], P('pipe'), may hold values from 0.5 to 1.5
- query_key_value_weight: bfloat16 [8, 2688, 16, 512], P('pipe', None, 'tensor'), may hold values from -0.125 to 0.125
- q_gain: float32 [8, 128], P('pipe'), may hold values from 0.5 to 1.5
- k_gain: float32 [8, 128], P('pipe'), may hold values from 0.5 to 1.5
- cached_key_rows: bfloat16 [8, 16, 1024, 128], P('pipe', 'tensor'), may hold values from -3 to 3
- cached_value_rows: bfloat16 [8, 16, 1024, 128], P('pipe', 'tensor'), may hold values from -6 to 6
- w_out: bfloat16 [8, 4096, 2688], P('pipe', 'tensor'), may hold values from -0.09375 to 0.09375
- post_gain: float32 [8, 2688], P('pipe'), may hold values from 0.5 to 1.5
Outputs:
- hidden: bfloat16 [8, 2, 512, 2688], P('pipe', None, 'tensor')
The draws below stay inside these ranges and needn't reach their ends.
All inputs are finite; a program needn't handle non-finite values.
Results may differ from the reference program's by a relative error of at most 0.015.
Values may be sent and summed in bfloat16 or wider, within the bound.
No kernel may reach another device: no remote copies, remote signals or barrier semaphores. Data moves between devices by JAX's collectives and lax.ppermute only.
A program may use at most 128 MiB of HBM per device.

```python
import math
import jax
import jax.numpy as jnp
from jax import lax

MODEL_DIM = 2688
HQ = 32
KEY_VALUE_HEADS = 16
HEAD_SIZE = 128
WINDOW_LENGTH = 1024
TICKS = 2
ROWS = 512
QUERY_PER_KEY = 2
LAYER_COUNT = 8
N_TENSOR = 4


def levels(rng, extent, shards, low, top_value):
    def one(dim, blocks):
        heights = jax.random.uniform(jax.random.fold_in(jax.random.fold_in(rng, 6), dim), (blocks,), jnp.float32, low / len(shards), top_value / len(shards))
        return jnp.repeat(jnp.exp(heights), extent[dim] // blocks).reshape((-1,) + (1,) * (len(extent) - dim - 1))

    factor_of = one(*shards[0])
    for cut in shards[1:]:
        factor_of = factor_of * one(*cut)
    return factor_of


def noise(own_key, extent, scale, bound, split=(), kind=jnp.bfloat16):
    level = levels(own_key, extent, split, -0.22, 0.18) if split else 1.0
    result = jax.random.normal(own_key, extent, jnp.float32) * scale * level
    return jnp.minimum(jnp.maximum(result, -bound), bound).astype(kind)


def setup_inputs(seed: int = 0) -> dict:
    keys = jax.random.split(jax.random.key(seed), 12)
    return {
        "held_rows": noise(keys[0], (LAYER_COUNT, ROWS, MODEL_DIM), 1.0, 6.0, ((0, 8), (1, 4))),
        "incoming": noise(keys[1], (TICKS - 1, ROWS, MODEL_DIM), 1.0, 6.0, ((1, 4),)),
        "first_position": jax.random.randint(keys[2], (1,), 0, WINDOW_LENGTH // 2).astype(jnp.int32),
        "in_gain": jnp.clip(1.0 + 0.1 * jax.random.normal(keys[3], (LAYER_COUNT, MODEL_DIM), jnp.float32), 0.5, 1.5),
        "query_key_value_weight": noise(keys[4], (LAYER_COUNT, MODEL_DIM, KEY_VALUE_HEADS, (QUERY_PER_KEY + 2) * HEAD_SIZE), MODEL_DIM ** -0.5, 0.125, ((0, 8), (2, 4))),
        "q_gain": jnp.clip(1.0 + 0.1 * jax.random.normal(keys[5], (LAYER_COUNT, HEAD_SIZE), jnp.float32), 0.5, 1.5),
        "k_gain": jnp.clip(1.0 + 0.1 * jax.random.normal(keys[6], (LAYER_COUNT, HEAD_SIZE), jnp.float32), 0.5, 1.5),
        "cached_key_rows": noise(keys[7], (LAYER_COUNT, KEY_VALUE_HEADS, WINDOW_LENGTH, HEAD_SIZE), 1.0, 3.0, ((0, 8), (1, 4))),
        "cached_value_rows": noise(keys[8], (LAYER_COUNT, KEY_VALUE_HEADS, WINDOW_LENGTH, HEAD_SIZE), 1.0, 6.0, ((0, 8), (1, 4))),
        "w_out": noise(keys[9], (LAYER_COUNT, HQ * HEAD_SIZE, MODEL_DIM), (HQ * HEAD_SIZE) ** -0.5, 0.09375, ((0, 8), (1, 4))),
        "post_gain": jnp.clip(1.0 + 0.1 * jax.random.normal(keys[10], (LAYER_COUNT, MODEL_DIM), jnp.float32), 0.5, 1.5),
    }


query_scale = 168.0 ** (-0.5)
norm_eps = 1e-06
rope_base = 10000.0

def rms_scale(values, gain_vec):
    mean_square = lax.optimization_barrier(jnp.mean(values * values, axis=-1, keepdims=True))
    return values * lax.rsqrt(mean_square + norm_eps) * gain_vec

def rotate(values, positions):
    half_width = values.shape[-1] // 2
    frequency = jnp.exp(jnp.arange(half_width, dtype=jnp.float32) * (-math.log(rope_base) / half_width))
    angles = positions.astype(jnp.float32)[:, None] * frequency[None, :]
    angles = angles.reshape((angles.shape[0],) + (1,) * (values.ndim - 2) + (half_width,))
    cosine = jnp.cos(angles)
    sine_part = jnp.sin(angles)
    first_half = values[..., :half_width]
    second = values[..., half_width:]
    return jnp.concatenate([first_half * cosine - second * sine_part, second * cosine + first_half * sine_part], axis=-1)

def apply_layer(inputs, in_gain, query_key_value_weight, q_gain, k_gain, w_out, post_gain, prev_keys, prev_values, start_pos):
    row_total = inputs.shape[0]
    scaled = (inputs.astype(jnp.float32) * in_gain).astype(jnp.bfloat16)
    projected_rows = jnp.dot(scaled, query_key_value_weight.reshape(MODEL_DIM, -1), preferred_element_type=jnp.float32)
    projected_rows = projected_rows.reshape(row_total, KEY_VALUE_HEADS, QUERY_PER_KEY + 2, HEAD_SIZE)
    query_pos = start_pos + jnp.arange(row_total, dtype=jnp.int32)
    queries = rotate(rms_scale(projected_rows[:, :, :QUERY_PER_KEY], q_gain), query_pos).astype(jnp.bfloat16)
    key_rows = rotate(rms_scale(projected_rows[:, :, QUERY_PER_KEY], k_gain), query_pos).astype(jnp.bfloat16)
    value_rows = projected_rows[:, :, QUERY_PER_KEY + 1].astype(jnp.bfloat16)
    key_heads = jnp.swapaxes(key_rows, 0, 1)
    value_heads = jnp.swapaxes(value_rows, 0, 1)
    all_keys = jnp.concatenate([prev_keys, key_heads], axis=1)
    all_values = jnp.concatenate([prev_values, value_heads], axis=1)
    prev_length = prev_keys.shape[1]
    key_pos = start_pos - prev_length + jnp.arange(prev_length + row_total, dtype=jnp.int32)
    visible = (key_pos[None, :] <= query_pos[:, None]) & (key_pos[None, :] > query_pos[:, None] - WINDOW_LENGTH) & (key_pos[None, :] >= 0)
    scores = jnp.einsum('rkgd,kld->kgrl', queries.astype(jnp.float32), all_keys.astype(jnp.float32)) * query_scale
    weights = jnp.where(visible[None, None], jnp.exp(scores), jnp.zeros_like(scores))
    totals = lax.optimization_barrier(jnp.sum(weights, axis=-1, keepdims=True))
    rounded = lax.optimization_barrier(weights.astype(jnp.bfloat16))
    mixed_heads = jnp.einsum('kgrl,kld->kgrd', rounded.astype(jnp.float32), all_values.astype(jnp.float32)) / totals
    mixed_heads = jnp.transpose(mixed_heads.astype(jnp.bfloat16), (2, 0, 1, 3))
    grouped = mixed_heads.reshape(row_total, N_TENSOR, -1).astype(jnp.float32)
    w_grouped = w_out.reshape(N_TENSOR, -1, MODEL_DIM).astype(jnp.float32)
    partial_value = jnp.einsum('rtc,tcd->trd', grouped, w_grouped)
    partial_value = lax.optimization_barrier(partial_value.astype(jnp.bfloat16)).astype(jnp.float32)
    summed = lax.optimization_barrier(jnp.sum(partial_value, axis=0))
    hidden = (inputs.astype(jnp.float32) + rms_scale(summed, post_gain)).astype(jnp.bfloat16)
    return (hidden, key_heads, value_heads)

def one_section(operands):
    return apply_layer(*operands)

def reference(held_rows, incoming, first_position, in_gain, query_key_value_weight, q_gain, k_gain, cached_key_rows, cached_value_rows, w_out, post_gain):
    section_ids = jnp.arange(LAYER_COUNT, dtype=jnp.int32)
    inputs = held_rows
    prev_keys = cached_key_rows
    prev_values = cached_value_rows
    outputs = []
    for micro_step in range(TICKS):
        starts = first_position[0] + (LAYER_COUNT - 1 - section_ids + micro_step) * ROWS
        hidden, key_heads, value_heads = lax.map(one_section, (inputs, in_gain, query_key_value_weight, q_gain, k_gain, w_out, post_gain, prev_keys, prev_values, starts))
        outputs.append(hidden)
        if micro_step + 1 < TICKS:
            inputs = jnp.concatenate([incoming[micro_step][None], hidden[:-1]], axis=0)
            prev_keys = jnp.concatenate([prev_keys, key_heads], axis=2)
            prev_values = jnp.concatenate([prev_values, value_heads], axis=2)
    return jnp.stack(outputs, axis=1)
```

```python
import functools
import math

import jax
import jax.numpy as jnp
from jax import lax
from jax.experimental import pallas as pl
from jax.experimental.pallas import tpu as pltpu
from jax.sharding import PartitionSpec as P

TICKS = 2

query_scale = 168.0 ** (-0.5)
norm_eps = 1e-06
rope_base = 10000.0


def exchange(block, bit):
    devices = range(lax.axis_size("tensor"))
    return lax.ppermute(block, "tensor", [(i, i ^ bit) for i in devices])


def shifted(block, axis, distance):
    devices = range(lax.axis_size(axis))
    route = [(i - distance, i) for i in devices if i - distance in devices]
    return lax.ppermute(block, axis, route)


def bit_orders():
    count = lax.axis_size("tensor").bit_length() - 1
    bits = [1 << b for b in range(count)]
    return (bits, bits[::-1])


def gather_blocks(halves):
    held = [{0: half} for half in halves]
    for step in range(len(bit_orders()[0])):
        for path, order in enumerate(bit_orders()):
            bit = order[step]
            for j in list(held[path]):
                held[path][j ^ bit] = exchange(held[path][j], bit)
    return {j: [path[j] for path in held] for j in held[0]}


def scatter_sum(partial_rows):
    sums = []
    for path, order in enumerate(bit_orders()):
        terms = {j: halves[path] for j, halves in partial_rows.items()}
        own = terms.pop(0).astype(jnp.float32)
        for bit in order:
            leaving = [j for j in terms if j & bit]
            for j in sorted(leaving, reverse=True):
                arrived = exchange(terms.pop(j), bit).astype(jnp.float32)
                if j == bit:
                    own = own + arrived
                else:
                    terms[j ^ bit] = (terms[j ^ bit].astype(jnp.float32) + arrived).astype(jnp.bfloat16)
        sums.append(own)
    return sums


def whole_spec(array):
    return pl.BlockSpec(array.shape, lambda k, *_: (0,) * array.ndim)


def head_spec(array):
    return pl.BlockSpec((1,) + array.shape[1:], lambda k, *_: (k,) + (0,) * (array.ndim - 1))


def project_kernel(block_count, place_ref, *refs):
    row_refs, refs = refs[: 2 * block_count], refs[2 * block_count :]
    w_ref, cos_ref, sin_ref, q_gain_ref, k_gain_ref = refs[:5]
    out_refs = refs[5:]
    head = cos_ref.shape[1]
    group = w_ref.shape[2] // head - 2
    size = 2 * row_refs[0].shape[0]
    rows = jnp.concatenate([ref[...] for ref in row_refs], axis=0)
    projected = jnp.dot(rows, w_ref[0], preferred_element_type=jnp.float32)
    for i in range(block_count):
        q_ref, k_ref, v_ref = out_refs[3 * i : 3 * i + 3]
        at = pl.ds(pl.multiple_of(place_ref[i], size), size)
        cosine, sine = cos_ref[at, :], sin_ref[at, :]
        block = projected[i * size : (i + 1) * size]

        def turned(values, gain):
            mean_square = jnp.mean(values * values, axis=-1, keepdims=True)
            values = values * lax.rsqrt(mean_square + norm_eps) * gain
            return values * cosine + pltpu.roll(values, head // 2, 1) * sine

        for g in range(group):
            q_ref[0, g] = turned(block[:, g * head : (g + 1) * head], q_gain_ref[...]).astype(q_ref.dtype)
        k_ref[0] = turned(block[:, group * head : (group + 1) * head], k_gain_ref[...]).astype(k_ref.dtype)
        v_ref[0] = block[:, (group + 1) * head :].astype(v_ref.dtype)


def project(blocks, places, w_heads, cosine, sine, q_scale, k_scale):
    kv_local, model_width, width = w_heads.shape
    head = cosine.shape[1]
    group = width // head - 2
    size = 2 * blocks[0][0].shape[0]
    rows = [half for block in blocks for half in block]
    out_shape, out_specs = [], []
    for _ in blocks:
        for shape in ((kv_local, group, size, head), (kv_local, size, head), (kv_local, size, head)):
            out_shape.append(jax.ShapeDtypeStruct(shape, jnp.bfloat16))
            out_specs.append(head_spec(out_shape[-1]))
    operands = rows + [w_heads, cosine, sine, q_scale, k_scale]
    in_specs = [whole_spec(a) for a in operands]
    in_specs[len(rows)] = head_spec(w_heads)
    total = size * len(blocks)
    out = pl.pallas_call(
        functools.partial(project_kernel, len(blocks)),
        grid_spec=pltpu.PrefetchScalarGridSpec(
            num_scalar_prefetch=1, grid=(kv_local,), in_specs=in_specs, out_specs=out_specs
        ),
        out_shape=out_shape,
        compiler_params=pltpu.CompilerParams(vmem_limit_bytes=32 << 20),
        cost_estimate=pl.CostEstimate(
            flops=2 * total * model_width * width * kv_local,
            bytes_accessed=2 * (w_heads.size + total * (model_width + width * kv_local)),
            transcendentals=0,
        ),
    )(jnp.stack(places), *operands)
    return [tuple(out[3 * i : 3 * i + 3]) for i in range(len(blocks))]


def attend_kernel(new_count, place_ref, *refs):
    q_ref, old_k_ref, old_v_ref, valid_ref = refs[:4]
    k_refs = refs[4 : 4 + new_count]
    v_refs = refs[4 + new_count : 4 + 2 * new_count]
    w_ref, first_ref, second_ref, key_list, value_list, mixed = refs[4 + 2 * new_count :]
    step = pl.program_id(0)
    kv_local, size, _ = mixed.shape
    group, _, head = q_ref.shape[1:]
    window = old_k_ref.shape[1]
    key_list[:window] = old_k_ref[0]
    value_list[:window] = old_v_ref[0] * valid_ref[:window]
    for i in range(new_count):
        at = pl.ds(pl.multiple_of(place_ref[1 + i], size), size)
        key_list[at, :] = k_refs[i][0]
        value_list[at, :] = v_refs[i][0]
    seen = pl.ds(pl.multiple_of(place_ref[0], size), window + size)
    queries = q_ref[0].reshape(group * size, head)
    scores = lax.dot_general(
        queries, key_list[seen, :], (((1,), (1,)), ((), ())), preferred_element_type=jnp.float32
    )
    factor = query_scale * math.log2(math.e)
    if size % head == 0:
        row = lax.rem(lax.broadcasted_iota(jnp.int32, (group * size, size), 0), size)
        late = lax.broadcasted_iota(jnp.int32, (group * size, size), 1) <= row
        edge = jnp.exp2(jnp.where(late, scores[:, window:], scores[:, :size]) * factor)
        middle = jnp.exp2(scores[:, size:window] * factor)
        weights = jnp.concatenate(
            [
                jnp.where(late, 0.0, edge).astype(jnp.bfloat16),
                middle.astype(jnp.bfloat16),
                jnp.where(late, edge, 0.0).astype(jnp.bfloat16),
            ],
            axis=1,
        )
    else:
        row = lax.rem(lax.broadcasted_iota(jnp.int32, scores.shape, 0), size)
        column = lax.broadcasted_iota(jnp.int32, scores.shape, 1)
        visible = (column > row) & (column <= row + window)
        weights = jnp.where(visible, jnp.exp2(scores * factor), 0.0).astype(jnp.bfloat16)
    values = jnp.concatenate([value_list[seen, :], valid_ref[seen, :]], axis=1)
    sums = jnp.dot(weights, values, preferred_element_type=jnp.float32)
    heads = (sums[:, :head] / sums[:, head:]).astype(jnp.bfloat16)
    mixed[step] = jnp.concatenate([heads[g * size : (g + 1) * size] for g in range(group)], axis=1)

    @pl.when(step == kv_local - 1)
    def _():
        rows = jnp.concatenate([mixed[i] for i in range(kv_local)], axis=1)
        term = jnp.dot(rows, w_ref[...], preferred_element_type=jnp.float32).astype(jnp.bfloat16)
        first_ref[...] = term[: size // 2]
        second_ref[...] = term[size // 2 :]


def attend(queries, old_keys, old_values, valid, keys, values, places, w_local):
    kv_local, group, size, head = queries.shape
    window = old_keys.shape[1]
    model_width = w_local.shape[1]
    operands = [queries, old_keys, old_values, valid, *keys, *values, w_local]
    in_specs = [head_spec(a) for a in operands]
    in_specs[3], in_specs[-1] = whole_spec(valid), whole_spec(w_local)
    half = jax.ShapeDtypeStruct((size // 2, model_width), jnp.bfloat16)
    listed = window + size * len(keys)
    return pl.pallas_call(
        functools.partial(attend_kernel, len(keys)),
        grid_spec=pltpu.PrefetchScalarGridSpec(
            num_scalar_prefetch=1,
            grid=(kv_local,),
            in_specs=in_specs,
            out_specs=[whole_spec(half)] * 2,
            scratch_shapes=[
                pltpu.VMEM((listed, head), jnp.bfloat16),
                pltpu.VMEM((listed, head), jnp.bfloat16),
                pltpu.VMEM((kv_local, size, group * head), jnp.bfloat16),
            ],
        ),
        out_shape=[half] * 2,
        compiler_params=pltpu.CompilerParams(vmem_limit_bytes=32 << 20),
        cost_estimate=pl.CostEstimate(
            flops=2 * size * kv_local * group * head * (3 * (window + size) + model_width),
            bytes_accessed=2 * (w_local.size + 2 * kv_local * listed * head),
            transcendentals=size * kv_local * group * window,
        ),
    )(jnp.stack(places), *operands)


def rms_scale(values, gain_vec):
    mean_square = jnp.mean(values * values, axis=-1, keepdims=True)
    return values * lax.rsqrt(mean_square + norm_eps) * gain_vec


def shards(
    held_rows,
    incoming,
    first_position,
    in_gain,
    query_key_value_weight,
    q_gain,
    k_gain,
    cached_key_rows,
    cached_value_rows,
    w_out,
    post_gain,
):
    section_id = lax.axis_index("pipe")
    section_count = lax.axis_size("pipe")
    index = lax.axis_index("tensor")
    size = held_rows.shape[1]
    rows = size * lax.axis_size("tensor")
    old_keys, old_values = cached_key_rows[0], cached_value_rows[0]
    window, head = old_keys.shape[1:]
    post_scale = post_gain[0]
    w_local = w_out[0]

    start = first_position[0] + (section_count - 1 - section_id) * rows
    frequency = jnp.exp(
        jnp.arange(head // 2, dtype=jnp.float32) * (-math.log(rope_base) / (head // 2))
    )
    positions = start + jnp.arange(TICKS * rows, dtype=jnp.int32)
    angles = positions.astype(jnp.float32)[:, None] * frequency[None, :]
    cosine, sine = jnp.cos(angles), jnp.sin(angles)
    cosine = jnp.concatenate([cosine, cosine], axis=1)
    sine = jnp.concatenate([-sine, sine], axis=1)
    key_places = start - window + jnp.arange(window + TICKS * rows, dtype=jnp.int32)
    valid = jnp.broadcast_to((key_places >= 0)[:, None], (key_places.shape[0], head)).astype(jnp.bfloat16)
    w_heads = jnp.swapaxes(
        (query_key_value_weight[0].astype(jnp.float32) * in_gain[0][:, None, None]).astype(jnp.bfloat16), 0, 1
    )

    halved = lambda block: [block[: size // 2], block[size // 2 :]]
    place = lambda j, tick: tick * rows + (index ^ j) * size
    keys, values, key_at = [], [], []
    outputs = []
    current = halved(held_rows[0])
    for tick in range(TICKS):
        blocks = gather_blocks(current)
        queries = {}
        for distance in range(len(bit_orders()[0]) + 1):
            near = [j for j in blocks if j.bit_count() == distance]
            made = project(
                [blocks[j] for j in near],
                [place(j, tick) for j in near],
                w_heads,
                cosine,
                sine,
                q_gain,
                k_gain,
            )
            for j, (block_queries, block_keys, block_values) in zip(near, made):
                queries[j] = block_queries
                keys.append(block_keys)
                values.append(block_values)
                key_at.append(window + place(j, tick))
        terms = {}
        for j in sorted(queries, key=lambda j: -j.bit_count()):
            terms[j] = attend(
                queries[j], old_keys, old_values, valid, keys, values, [place(j, tick)] + key_at, w_local
            )
        summed = scatter_sum(terms)
        hidden = [
            (own.astype(jnp.float32) + rms_scale(total, post_scale)).astype(jnp.bfloat16)
            for own, total in zip(current, summed)
        ]
        outputs += hidden
        if tick + 1 < TICKS:
            current = [
                jnp.where(section_id == 0, fresh, shifted(half, "pipe", 1))
                for fresh, half in zip(halved(incoming[tick]), hidden)
            ]
    return jnp.concatenate(outputs, axis=0).reshape(1, TICKS, size, -1)


def solution(mesh):
    return jax.shard_map(
        shards,
        mesh=mesh,
        in_specs=(
            P("pipe", "tensor", None),
            P(None, "tensor", None),
            P(),
            P("pipe", None),
            P("pipe", None, "tensor", None),
            P("pipe", None),
            P("pipe", None),
            P("pipe", "tensor", None, None),
            P("pipe", "tensor", None, None),
            P("pipe", "tensor", None),
            P("pipe", None),
        ),
        out_specs=P("pipe", None, "tensor", None),
        check_vma=False,
    )
```
